32 devices in a mesh: section: 4 (over y, x), dev: 8 (over z, core).
Axes of the slice: x: 2, y: 2, z: 4, core: 2. Of those that a mesh axis runs over, the one named last changes fastest.
Arguments:
- hidden: bfloat16 [256, 2048], P('dev'), may hold values from -8 to 8
- lengths: int32 [256], P('dev'), may hold values from 1 to 256, as said below
- attn_gain: float32 [2048], replicated, may hold values from 0.1 to 1.9
- w_query: bfloat16 [2048, 3072], P(None, 'section'), may hold values from -0.125 to 0.125
- w_latent: bfloat16 [2048, 512], replicated, may hold values from -0.125 to 0.125
- latent_gain: float32 [512], replicated, may hold values from 0.1 to 1.9
- w_rope_key: bfloat16 [64, 2048], replicated, may hold values from -0.125 to 0.125
- w_key_up: bfloat16 [16, 512, 128], P('section'), may hold values from -0.5 to 0.5
- w_value_up: bfloat16 [16, 512, 128], P('section'), may hold values from -0.25 to 0.25
- w_out: bfloat16 [2048, 2048], P('section'), may hold values from -0.125 to 0.125
- latent_cache: bfloat16 [256, 256, 512], P('dev'), may hold values from -6 to 6
- rope_cache: bfloat16 [256, 64, 256], P('dev'), may hold values from -1200 to 1200
- ffn_gain: float32 [2048], replicated, may hold values from 0.1 to 1.9
- expert_ids: int32 [256, 6], P('dev'), may hold values from 0 to 63, all different within a row; in each aligned block of 8 rows (0 to 7, 8 to 15, ...) at most 2 rows name the same one
- route_weights: float32 [256, 6], P('dev'), may hold values from 0.05 to 0.5
- w_gate_up: bfloat16 [64, 2, 1408, 2048], P('dev', None, 'section'), may hold values from -0.125 to 0.125
- w_down: bfloat16 [64, 1408, 2048], P('dev', 'section'), may hold values from -0.15625 to 0.15625
Outputs:
- layer_out: bfloat16 [256, 2048], P('dev')
The draws below stay inside these ranges and needn't reach their ends.
Inputs may be any that keep to these rules, and one draw needn't show every extreme that they name: `lengths`: every aligned block of 32 rows holds a row of length 256. `expert_ids`: each row names 6 different experts. In every aligned block of 8 rows no expert is named by more than 2 rows, and some block has an expert named by exactly 2.
All inputs are finite; a program needn't handle non-finite values.
Results may differ from the reference program's by a relative error of at most 0.011.
Values may be sent and summed in bfloat16 or wider, within the bound.
A program may use at most 128 MiB of HBM per device.

```python
import math
import jax
import jax.numpy as jnp
import numpy as np
from jax import lax

D = 2048
HEADS = 16
NOPE = 128
ROPE = 64
LATENT = 512
VHEAD = 128
FF = 1408
EXPERTS = 64
TOPK = 6
ROW_DEV = 32
LEN = 256
MOST = 2
ROWS = 256
ROW_Q = 8


def draw_hidden(key, part):
    base_key, row_key, column_key = jax.random.split(jax.random.fold_in(key, 11), 3)
    row_scale = jnp.exp(jax.random.uniform(row_key, (ROWS, 1), jnp.float32, math.log(0.2), math.log(2.0)))
    column_scale = jnp.exp(jax.random.uniform(column_key, (1, D), jnp.float32, math.log(0.3), math.log(3.0)))
    values = jax.random.normal(base_key, (ROWS, D), jnp.float32)
    return jnp.clip(values * row_scale * column_scale, -8.0, 8.0).astype(jnp.bfloat16)


def draw_lengths(key, part):
    length_key, pick_key = jax.random.split(jax.random.fold_in(key, 23))
    values = jax.random.randint(length_key, (ROWS,), 1, LEN + 1, dtype=jnp.int32)
    chosen = jax.random.randint(pick_key, (ROWS // ROW_DEV,), 0, ROW_DEV, dtype=jnp.int32)
    positions = jnp.arange(ROWS, dtype=jnp.int32)
    full_row = positions % ROW_DEV == chosen[positions // ROW_DEV]
    return jnp.where(full_row, LEN, values).astype(jnp.int32)


def draw_rope_cache(key, part):
    base_key = jax.random.fold_in(jax.random.fold_in(key, 37), 0)
    values = jnp.clip(jax.random.normal(base_key, (ROWS, ROPE, LEN), jnp.float32), -6.0, 6.0)
    return jnp.clip(values, -1200.0, 1200.0).astype(jnp.bfloat16)


def steps_of(rng, extent, cuts, low, top_value):
    level = 1.0
    for dim, blocks in cuts:
        draws = jax.random.uniform(jax.random.fold_in(jax.random.fold_in(rng, 6), dim), (blocks,), jnp.float32, low / len(cuts), top_value / len(cuts))
        level = level * jnp.repeat(jnp.exp(draws), extent[dim] // blocks).reshape((-1,) + (1,) * (len(extent) - 1 - dim))
    return level


def routed_block(stream_key, own, number, rows, number_of, top, limit, lean):
    ranking = jax.random.permutation(stream_key, number_of)
    heavy_load, usual = load_shares(number_of, rows * top, limit, lean, True), load_shares(number_of, rows * top, limit, lean, False)
    places = jnp.arange(number_of)

    def named(sizes, turn):
        used = int((sizes > 0).sum())
        fixed = max(1, used // 4)
        passed = fixed + (places - fixed + turn * (used - fixed)) % max(1, number_of - fixed)
        return jnp.zeros((number_of,), jnp.int32).at[ranking[jnp.where(places < fixed, places, passed)]].set(jnp.asarray(sizes, jnp.int32))

    sizes = jnp.where(number % 4 == 0, named(heavy_load, number // 4), named(usual, number - number // 4 - 1))
    mixed = jax.random.permutation(jax.random.fold_in(own, 3), number_of)
    donor, taker = mixed[0:number_of // 2 * 2:2], mixed[1:number_of // 2 * 2:2]
    slack = jnp.minimum(sizes[donor] - 1, limit - sizes[taker]) // 2
    slack = jnp.where((donor == ranking[0]) | (taker == ranking[0]) | (sizes[taker] == 0), 0, jnp.maximum(slack, 0))
    passed = jax.random.randint(jax.random.fold_in(own, 4), (number_of // 2,), 0, 1 << 20) % (slack + 1)
    sizes = sizes.at[donor].add(-passed).at[taker].add(passed)
    items = jnp.searchsorted(jnp.cumsum(sizes), jnp.arange(rows * top), side="right").astype(jnp.int32)
    grid = items.reshape(top, rows).T
    grid = grid[jax.random.permutation(jax.random.fold_in(own, 1), rows)]
    turn = jax.random.randint(jax.random.fold_in(own, 2), (rows, 1), 0, top)
    return jnp.take_along_axis(grid, (jnp.arange(top)[None, :] + turn) % top, axis=1)


def load_shares(amount, total, bound, lean, full):
    weights = [(1 << 20) // math.isqrt(rank ** lean) + 1 for rank in range(1, amount + 1)]
    largest = bound if full else min(bound, max(-(-total // amount), total * weights[0] // sum(weights)))
    least = 1 if total - largest >= amount - 1 else 0
    holding, spare = [largest] + [least] * (amount - 1), total - largest - least * (amount - 1)
    while spare > 0:
        free = [i for i in range(1, amount) if holding[i] < largest] or [i for i in range(1, amount) if holding[i] < bound]
        mass, budget = sum([weights[i] for i in free]), spare
        for i in free:
            more = min(bound - holding[i], max(1, budget * weights[i] // mass), spare)
            holding[i] = holding[i] + more
            spare = spare - more
    return np.array(holding)


def gaussian(stream_key, extent, deviation, reach, cuts=(), held_as=jnp.bfloat16):
    array = deviation * jax.random.normal(stream_key, extent, jnp.float32)
    if cuts:
        array = array * steps_of(stream_key, extent, cuts, -0.22, 0.18)
    return jnp.clip(array, -reach, reach).astype(held_as)


def setup_inputs(seed: int = 0) -> dict:
    splits = jax.random.split(jax.random.key(seed), 18)
    hidden = draw_hidden(jax.random.fold_in(splits[17], 71), 0)
    lengths = draw_lengths(jax.random.fold_in(splits[17], 71), 0)
    attn_gain = jnp.clip(1.0 + 0.18 * jax.random.normal(splits[2], (D,), jnp.float32), 0.1, 1.9)
    w_query = gaussian(splits[3], (D, HEADS * (NOPE + ROPE)), D ** -0.5, 0.125, ((1, 4),))
    w_latent = gaussian(splits[4], (D, LATENT), D ** -0.5, 0.125)
    latent_gain = jnp.clip(1.0 + 0.18 * jax.random.normal(splits[5], (LATENT,), jnp.float32), 0.1, 1.9)
    w_rope_key = gaussian(splits[6], (ROPE, D), D ** -0.5, 0.125)
    w_key_up = gaussian(splits[7], (HEADS, LATENT, NOPE), NOPE ** -0.5, 0.5, ((0, 4),))
    w_value_up = gaussian(splits[8], (HEADS, LATENT, VHEAD), LATENT ** -0.5, 0.25, ((0, 4),))
    w_out = gaussian(splits[9], (HEADS * VHEAD, D), (HEADS * VHEAD) ** -0.5, 0.125, ((0, 4),))
    latent_cache = gaussian(splits[10], (ROWS, LEN, LATENT), 1.0, 6.0, ((0, 8),))
    rope_cache = draw_rope_cache(jax.random.fold_in(splits[17], 71), 0)
    ffn_gain = jnp.clip(1.0 + 0.18 * jax.random.normal(splits[12], (D,), jnp.float32), 0.1, 1.9)
    expert_ids_keys = jax.random.split(jax.random.fold_in(splits[13], 1), ROWS // ROW_Q)
    expert_ids_turns = jax.random.permutation(jax.random.fold_in(splits[13], 3), ROWS // ROW_Q)
    expert_ids = jax.vmap(lambda own, number: routed_block(jax.random.fold_in(splits[13], 2), own, number, ROW_Q, EXPERTS, TOPK, MOST, 2))(expert_ids_keys, expert_ids_turns).reshape((ROWS, TOPK))
    route_weights = jnp.clip(jnp.exp(math.log(0.5) - 2.3025851 * jax.random.uniform(splits[14], (ROWS, TOPK), jnp.float32) ** steps_of(splits[14], (ROWS, TOPK), ((0, 8),), -0.2, 0.2)), 0.05, 0.5)
    w_gate_up = gaussian(splits[15], (EXPERTS, 2, FF, D), D ** -0.5, 0.125, ((0, 8), (2, 4)))
    w_down = gaussian(splits[16], (EXPERTS, FF, D), FF ** -0.5, 0.15625, ((0, 8), (1, 4)))
    return dict(hidden=hidden, lengths=lengths, attn_gain=attn_gain, w_query=w_query, w_latent=w_latent, latent_gain=latent_gain, w_rope_key=w_rope_key, w_key_up=w_key_up, w_value_up=w_value_up, w_out=w_out, latent_cache=latent_cache, rope_cache=rope_cache, ffn_gain=ffn_gain, expert_ids=expert_ids, route_weights=route_weights, w_gate_up=w_gate_up, w_down=w_down)


epsilon = 1e-06
far_below = -1e+30

def rms_norm(values, norm_gain):
    mean_square = lax.optimization_barrier(jnp.mean(values * values, axis=-1, keepdims=True))
    return values * lax.rsqrt(mean_square + epsilon) * norm_gain

def rotary(values, positions):
    half_width = values.shape[-1] // 2
    step_index = jnp.arange(half_width, dtype=jnp.float32)
    frequency = jnp.exp(-jnp.log(10000.0) * step_index / half_width)
    angles = positions.astype(jnp.float32)[:, None] * frequency[None, :]
    if values.ndim == 3:
        angles = angles[:, None, :]
    cosine = jnp.cos(angles)
    sine_part = jnp.sin(angles)
    first_half = values[..., :half_width]
    second = values[..., half_width:]
    return jnp.concatenate([first_half * cosine - second * sine_part, second * cosine + first_half * sine_part], axis=-1)

def slot_targets(expert_ids, block_rows):
    row_count, top_count = expert_ids.shape
    blocks = row_count // block_rows
    flat_ids = expert_ids.reshape(blocks, block_rows * top_count)
    onehot = (flat_ids[:, :, None] == jnp.arange(EXPERTS, dtype=jnp.int32)[None, None, :]).astype(jnp.int32)
    earlier = jnp.cumsum(onehot, axis=1) - onehot
    rank_in = lax.optimization_barrier(jnp.sum(earlier * onehot, axis=2))
    capacity = blocks * MOST
    target = flat_ids * capacity + jnp.arange(blocks, dtype=jnp.int32)[:, None] * MOST + rank_in
    return (target.reshape(row_count, top_count).astype(jnp.int32), capacity)

def attend(query_latent, query_rope, latent_new, key_new, latent_cache, rope_cache, lengths, score_scale):
    scores = jnp.einsum('rhl,rtl->rht', query_latent.astype(jnp.float32), latent_cache.astype(jnp.float32))
    scores = scores + jnp.einsum('rhp,rpt->rht', query_rope.astype(jnp.float32), rope_cache.astype(jnp.float32))
    scores = scores * score_scale
    self_score = jnp.einsum('rhl,rl->rh', query_latent.astype(jnp.float32), latent_new.astype(jnp.float32))
    self_score = (self_score + jnp.einsum('rhp,rp->rh', query_rope.astype(jnp.float32), key_new.astype(jnp.float32))) * score_scale
    places = jnp.arange(latent_cache.shape[1], dtype=jnp.int32)
    valid_mask = places[None, None, :] < lengths[:, None, None]
    masked = jnp.where(valid_mask, scores, far_below)
    peak_score = jnp.maximum(lax.optimization_barrier(jnp.max(masked, axis=2)), self_score)
    weights = jnp.where(valid_mask, jnp.exp(masked - peak_score[:, :, None]), 0.0)
    self_weight = jnp.exp(self_score - peak_score)
    totals = lax.optimization_barrier(jnp.sum(weights, axis=2)) + self_weight
    prob_cache = (weights / totals[:, :, None]).astype(jnp.bfloat16)
    prob_self = (self_weight / totals).astype(jnp.bfloat16)
    mixed = jnp.einsum('rht,rtl->rhl', prob_cache.astype(jnp.float32), latent_cache.astype(jnp.float32))
    mixed = mixed + prob_self.astype(jnp.float32)[:, :, None] * latent_new.astype(jnp.float32)[:, None, :]
    return mixed.astype(jnp.bfloat16)

def reference(hidden, lengths, attn_gain, w_query, w_latent, latent_gain, w_rope_key, w_key_up, w_value_up, w_out, latent_cache, rope_cache, ffn_gain, expert_ids, route_weights, w_gate_up, w_down):
    normed = rms_norm(hidden.astype(jnp.float32), attn_gain).astype(jnp.bfloat16)
    queries = jnp.dot(normed, w_query, preferred_element_type=jnp.float32).astype(jnp.bfloat16)
    queries = queries.reshape(ROWS, HEADS, NOPE + ROPE)
    query_rope = rotary(queries[:, :, NOPE:].astype(jnp.float32), lengths).astype(jnp.bfloat16)
    query_latent = jnp.einsum('rhn,hln->rhl', queries[:, :, :NOPE].astype(jnp.float32), w_key_up.astype(jnp.float32)).astype(jnp.bfloat16)
    latent_new = rms_norm(jnp.dot(normed, w_latent, preferred_element_type=jnp.float32), latent_gain).astype(jnp.bfloat16)
    key_raw = lax.dot_general(normed, w_rope_key, (((1,), (1,)), ((), ())), preferred_element_type=jnp.float32)
    key_new = rotary(key_raw, lengths).astype(jnp.bfloat16)
    score_scale = (NOPE + ROPE) ** (-0.5)
    block_count = ROWS // ROW_DEV

    def one_block(pieces):
        q_lat, q_rot, lat_new, k_new, lat_cache, rot_cache, lens = pieces
        mixed_latent = attend(q_lat, q_rot, lat_new, k_new, lat_cache, rot_cache, lens, score_scale)
        head_out = jnp.einsum('rhl,hlv->rhv', mixed_latent.astype(jnp.float32), w_value_up.astype(jnp.float32))
        return head_out.astype(jnp.bfloat16).reshape(ROW_DEV, HEADS * VHEAD)
    head_out = lax.map(one_block, (query_latent.reshape(block_count, ROW_DEV, HEADS, LATENT), query_rope.reshape(block_count, ROW_DEV, HEADS, ROPE), latent_new.reshape(block_count, ROW_DEV, LATENT), key_new.reshape(block_count, ROW_DEV, ROPE), latent_cache.reshape(block_count, ROW_DEV, LEN, LATENT), rope_cache.reshape(block_count, ROW_DEV, ROPE, LEN), lengths.reshape(block_count, ROW_DEV))).reshape(ROWS, HEADS * VHEAD)
    attention = jnp.dot(head_out, w_out, preferred_element_type=jnp.float32)
    middle = (hidden.astype(jnp.float32) + attention).astype(jnp.bfloat16)
    expert_in = rms_norm(middle.astype(jnp.float32), ffn_gain).astype(jnp.bfloat16)
    target, capacity = slot_targets(expert_ids, ROW_Q)
    row_ids = jnp.repeat(jnp.arange(ROWS, dtype=jnp.int32), TOPK)
    row_of = jnp.full((EXPERTS * capacity,), ROWS, jnp.int32).at[target.reshape(-1)].set(row_ids)
    padded = jnp.concatenate([expert_in, jnp.zeros((1, D), jnp.bfloat16)], axis=0)

    def one_expert(pieces):
        picked, gate_up, down_part = pieces
        rows_in = padded[picked]
        gate_part = jnp.dot(rows_in, gate_up[0].T, preferred_element_type=jnp.float32)
        up_part = jnp.dot(rows_in, gate_up[1].T, preferred_element_type=jnp.float32)
        activated = (jax.nn.silu(gate_part) * up_part).astype(jnp.bfloat16)
        return jnp.dot(activated, down_part, preferred_element_type=jnp.float32).astype(jnp.bfloat16)
    outputs = lax.map(one_expert, (row_of.reshape(EXPERTS, capacity), w_gate_up, w_down)).reshape(EXPERTS * capacity, D)
    routed = outputs[target.reshape(-1)].reshape(ROWS, TOPK, D).astype(jnp.float32)
    layer_out = middle.astype(jnp.float32) + lax.optimization_barrier(jnp.sum(route_weights[:, :, None] * routed, axis=1))
    return layer_out.astype(jnp.bfloat16)
```

```python
import functools

import jax
import jax.numpy as jnp
from jax import lax
from jax.experimental import pallas as pl
from jax.experimental.pallas import tpu as pltpu
from jax.sharding import PartitionSpec as P

MOST = 2
MESH = pl.DeviceIdType.MESH


epsilon = 1e-06
far_below = -1e30


def rms_norm(values, norm_gain):
    mean_square = jnp.mean(values * values, axis=-1, keepdims=True)
    return values * lax.rsqrt(mean_square + epsilon) * norm_gain


def rotary(values, positions):
    half_width = values.shape[-1] // 2
    step_index = jnp.arange(half_width, dtype=jnp.float32)
    frequency = jnp.exp(-jnp.log(10000.0) * step_index / half_width)
    angles = positions.astype(jnp.float32)[:, None] * frequency[None, :]
    if values.ndim == 3:
        angles = angles[:, None, :]
    cosine = jnp.cos(angles)
    sine_part = jnp.sin(angles)
    first_half = values[..., :half_width]
    second = values[..., half_width:]
    return jnp.concatenate(
        [first_half * cosine - second * sine_part, second * cosine + first_half * sine_part],
        axis=-1,
    )


def route_table(own_ids, own_weights, experts, block_index):
    hit = own_ids[:, :, None] == jnp.arange(experts, dtype=jnp.int32)[None, None, :]
    dense = jnp.sum(jnp.where(hit, own_weights[:, :, None], 0.0), axis=1)
    routed = jnp.any(hit, axis=1).astype(jnp.int32)
    rank = jnp.cumsum(routed, axis=0) - routed
    slot = jnp.where(routed > 0, block_index * MOST + rank, -1)
    return jnp.concatenate([dense, slot.astype(jnp.float32)], axis=1)


def expert_kernel(
    sections,
    devices,
    part_ref,
    hidden_ref,
    gain_ref,
    table_ref,
    w_up_ref,
    w_down_ref,
    out_ref,
    w_up,
    w_down,
    part_in,
    middle,
    row_out,
    rows_all,
    tables,
    pick,
    mix,
    packed,
    expert_out,
    sum_out,
    sum_in,
    own_out,
    finished,
    up_sem,
    down_sem,
    part_send,
    part_recv,
    table_send,
    table_recv,
    row_send,
    row_recv,
    sum_send,
    sum_recv,
    done_send,
    done_recv,
):
    section = lax.axis_index("section")
    dev = lax.axis_index("dev")
    total = sections * devices
    me = dev * sections + section
    local = w_up.shape[0]
    rows = total * row_out.shape[0]
    width = row_out.shape[1]
    experts = tables.shape[2] // 2
    slots = packed.shape[0] // local
    f32 = jnp.float32

    def up_copy(e):
        return pltpu.make_async_copy(w_up_ref.at[e], w_up.at[e], up_sem.at[e])

    def down_copy(e):
        return pltpu.make_async_copy(w_down_ref.at[e], w_down.at[e], down_sem.at[e])

    def place(t):
        return (lax.rem(t, sections), t // sections)

    def to_all(source, landing, send_sem, recv_sem):
        def copy(i, here):
            t = lax.rem(me + i, total)
            return pltpu.make_async_remote_copy(
                src_ref=source(t),
                dst_ref=landing.at[here],
                send_sem=send_sem.at[i],
                recv_sem=recv_sem.at[here],
                device_id=place(t),
                device_id_type=MESH,
            )

        @pl.loop(1, total)
        def _(i):
            copy(i, me).start()

        def wait_recv():
            @pl.loop(1, total)
            def _(i):
                copy(i, lax.rem(me + i, total)).wait_recv()

        def wait_send():
            @pl.loop(1, total)
            def _(i):
                copy(i, me).wait_send()

        return wait_recv, wait_send

    def to_sections(source, landing, send_sem, recv_sem):
        def copy(i, here):
            t = lax.rem(section + i, sections)
            return pltpu.make_async_remote_copy(
                src_ref=source(t),
                dst_ref=landing.at[here],
                send_sem=send_sem.at[i],
                recv_sem=recv_sem.at[here],
                device_id=(t, dev),
                device_id_type=MESH,
            )

        for i in range(1, sections):
            copy(i, section).start()

        def wait_recv():
            for i in range(1, sections):
                copy(i, lax.rem(section + i, sections)).wait_recv()

        def wait_send():
            for i in range(1, sections):
                copy(i, section).wait_send()

        return wait_recv, wait_send

    @pl.loop(0, local)
    def _(e):
        up_copy(e).start()
        down_copy(e).start()

    barrier = pltpu.get_barrier_semaphore()

    @pl.loop(1, total)
    def _(i):
        pl.semaphore_signal(
            barrier, inc=1, device_id=place(lax.rem(me + i, total)), device_id_type=MESH
        )

    pl.semaphore_wait(barrier, total - 1)

    part_recv_all, part_send_all = to_sections(
        lambda t: part_ref.at[t], part_in, part_send, part_recv
    )
    table_recv_all, table_send_all = to_all(lambda t: table_ref, tables, table_send, table_recv)
    part_in[section] = part_ref[section]
    tables[me] = table_ref[...]
    part_recv_all()
    summed = part_in[0]
    for j in range(1, sections):
        summed = summed + part_in[j]
    middle_rows = (hidden_ref[...].astype(f32) + summed).astype(jnp.bfloat16).astype(f32)
    middle[...] = middle_rows
    normed_rows = rms_norm(middle_rows, gain_ref[...]).astype(jnp.bfloat16)
    row_out[...] = normed_rows
    rows_all[me] = normed_rows
    row_recv_all, row_send_all = to_all(lambda t: row_out, rows_all, row_send, row_recv)

    table_recv_all()
    table = tables[...].reshape(rows, 2 * experts)
    lane = lax.broadcasted_iota(jnp.int32, (rows, 2 * experts), 1)
    column = lax.broadcasted_iota(jnp.int32, (rows, local * slots), 1)
    slot_at = jnp.full((rows, local * slots), -1.0, f32)
    weight_at = jnp.zeros((rows, local * slots), f32)
    for e in range(local):
        expert = dev * local + e
        weight_col = jnp.sum(jnp.where(lane == expert, table, 0.0), axis=1, keepdims=True)
        slot_col = jnp.sum(jnp.where(lane == experts + expert, table, 0.0), axis=1, keepdims=True)
        slot_col = jnp.where(slot_col < 0.0, -1.0, slot_col + float(e * slots))
        inside = (column >= e * slots) & (column < (e + 1) * slots)
        slot_at = jnp.where(inside, slot_col, slot_at)
        weight_at = jnp.where(inside, weight_col, weight_at)
    chosen = column.astype(f32) == slot_at
    pick[...] = jnp.where(chosen, 1.0, 0.0).astype(jnp.bfloat16)
    mix[...] = jnp.where(chosen, weight_at, 0.0).astype(jnp.bfloat16)

    row_recv_all()
    tile = 512

    @pl.loop(0, width // tile)
    def _(c):
        span = pl.ds(pl.multiple_of(c * tile, tile), tile)
        block = rows_all[:, :, span].astype(f32).reshape(rows, tile).astype(jnp.bfloat16)
        packed[:, span] = lax.dot_general(
            pick[...], block, (((0,), (0,)), ((), ())), preferred_element_type=f32
        ).astype(jnp.bfloat16)

    @pl.loop(0, local)
    def _(e):
        span = pl.ds(pl.multiple_of(e * slots, slots), slots)
        up_copy(e).wait()
        slot_rows = packed[span, :]
        flat = (((1,), (1,)), ((), ()))
        gate = lax.dot_general(slot_rows, w_up[e, 0], flat, preferred_element_type=f32)
        lift = lax.dot_general(slot_rows, w_up[e, 1], flat, preferred_element_type=f32)
        activated = (gate / (1.0 + jnp.exp(-gate)) * lift).astype(jnp.bfloat16)
        down_copy(e).wait()
        expert_out[span, :] = jnp.dot(
            activated, w_down[e], preferred_element_type=f32
        ).astype(jnp.bfloat16)

    @pl.loop(0, width // tile)
    def _(c):
        span = pl.ds(pl.multiple_of(c * tile, tile), tile)
        mixed = jnp.dot(mix[...], expert_out[:, span], preferred_element_type=f32)
        sum_out[:, :, span] = mixed.reshape(total, rows // total, tile).astype(jnp.bfloat16)

    sum_recv_all, sum_send_all = to_all(lambda t: sum_out.at[t], sum_in, sum_send, sum_recv)
    sum_in[me] = sum_out[me]
    part_send_all()
    table_send_all()
    row_send_all()
    sum_recv_all()
    result = (middle[...] + jnp.sum(sum_in[...].astype(f32), axis=0)).astype(jnp.bfloat16)
    own_out[...] = result
    finished[section] = result
    done_recv_all, done_send_all = to_sections(
        lambda t: own_out, finished, done_send, done_recv
    )
    sum_send_all()
    done_recv_all()
    out_ref[...] = finished[...]
    done_send_all()


def expert_layer(part, own_hidden, ffn_gain, table, w_gate_up, w_down):
    sections = lax.axis_size("section")
    devices = lax.axis_size("dev")
    total = sections * devices
    quarter, width = own_hidden.shape
    local, _, units, _ = w_gate_up.shape
    slots = total * MOST
    rows = total * quarter
    bf16, f32 = jnp.bfloat16, jnp.float32
    vmem = pl.BlockSpec(memory_space=pltpu.VMEM)
    anywhere = pl.BlockSpec(memory_space=pl.ANY)
    sems = lambda count: pltpu.SemaphoreType.DMA((count,))
    out = pl.pallas_call(
        functools.partial(expert_kernel, sections, devices),
        out_shape=jax.ShapeDtypeStruct((sections, quarter, width), bf16),
        in_specs=[vmem] * 4 + [anywhere] * 2,
        out_specs=vmem,
        scratch_shapes=[
            pltpu.VMEM(w_gate_up.shape, bf16),
            pltpu.VMEM(w_down.shape, bf16),
            pltpu.VMEM((sections, quarter, width), f32),
            pltpu.VMEM((quarter, width), f32),
            pltpu.VMEM((quarter, width), bf16),
            pltpu.VMEM((total, quarter, width), bf16),
            pltpu.VMEM((total,) + table.shape, f32),
            pltpu.VMEM((rows, local * slots), bf16),
            pltpu.VMEM((rows, local * slots), bf16),
            pltpu.VMEM((local * slots, width), bf16),
            pltpu.VMEM((local * slots, width), bf16),
            pltpu.VMEM((total, quarter, width), bf16),
            pltpu.VMEM((total, quarter, width), bf16),
            pltpu.VMEM((quarter, width), bf16),
            pltpu.VMEM((sections, quarter, width), bf16),
            sems(local),
            sems(local),
            sems(sections),
            sems(sections),
            sems(total),
            sems(total),
            sems(total),
            sems(total),
            sems(total),
            sems(total),
            sems(sections),
            sems(sections),
        ],
        compiler_params=pltpu.CompilerParams(
            collective_id=0, has_side_effects=True, vmem_limit_bytes=58 * 1024 * 1024
        ),
    )(
        part.reshape(sections, quarter, width),
        own_hidden,
        ffn_gain.reshape(1, width),
        table,
        w_gate_up,
        w_down,
    )
    return out.reshape(sections * quarter, width)


def attend(
    query_latent, query_rope, latent_new, key_new, latent_cache, rope_cache, lengths, score_scale
):
    scores = jnp.einsum(
        "rhl,rtl->rht", query_latent, latent_cache, preferred_element_type=jnp.float32
    )
    scores = scores + jnp.einsum(
        "rhp,rpt->rht", query_rope, rope_cache, preferred_element_type=jnp.float32
    )
    scores = scores * score_scale
    self_score = jnp.einsum(
        "rhl,rl->rh", query_latent, latent_new, preferred_element_type=jnp.float32
    )
    self_score = (
        self_score
        + jnp.einsum("rhp,rp->rh", query_rope, key_new, preferred_element_type=jnp.float32)
    ) * score_scale
    places = jnp.arange(latent_cache.shape[1], dtype=jnp.int32)
    valid_mask = places[None, None, :] < lengths[:, None, None]
    masked = jnp.where(valid_mask, scores, far_below)
    peak_score = jnp.maximum(jnp.max(masked, axis=2), self_score)
    weights = jnp.where(valid_mask, jnp.exp(masked - peak_score[:, :, None]), 0.0)
    self_weight = jnp.exp(self_score - peak_score)
    totals = jnp.sum(weights, axis=2) + self_weight
    prob_cache = (weights / totals[:, :, None]).astype(jnp.bfloat16)
    prob_self = (self_weight / totals).astype(jnp.bfloat16)
    mixed = jnp.einsum("rht,rtl->rhl", prob_cache, latent_cache, preferred_element_type=jnp.float32)
    mixed = (
        mixed
        + prob_self.astype(jnp.float32)[:, :, None] * latent_new.astype(jnp.float32)[:, None, :]
    )
    return mixed.astype(jnp.bfloat16)


def per_device(
    hidden,
    lengths,
    attn_gain,
    w_query,
    w_latent,
    latent_gain,
    w_rope_key,
    w_key_up,
    w_value_up,
    w_out,
    latent_cache,
    rope_cache,
    ffn_gain,
    expert_ids,
    route_weights,
    w_gate_up,
    w_down,
):
    sections = lax.axis_size("section")
    devices = lax.axis_size("dev")
    row_count = hidden.shape[0]
    quarter = row_count // sections
    head_local = w_key_up.shape[0]
    nope_width = w_key_up.shape[2]
    rope_width = w_rope_key.shape[0]
    score_scale = (nope_width + rope_width) ** (-0.5)
    normed = rms_norm(hidden.astype(jnp.float32), attn_gain).astype(jnp.bfloat16)
    queries = jnp.dot(normed, w_query, preferred_element_type=jnp.float32).astype(jnp.bfloat16)
    queries = queries.reshape(row_count, head_local, nope_width + rope_width)
    query_rope = rotary(queries[:, :, nope_width:].astype(jnp.float32), lengths).astype(
        jnp.bfloat16
    )
    query_latent = jnp.einsum(
        "rhn,hln->rhl", queries[:, :, :nope_width], w_key_up, preferred_element_type=jnp.float32
    ).astype(jnp.bfloat16)
    latent_new = rms_norm(
        jnp.dot(normed, w_latent, preferred_element_type=jnp.float32), latent_gain
    ).astype(jnp.bfloat16)
    key_raw = lax.dot_general(
        normed, w_rope_key, (((1,), (1,)), ((), ())), preferred_element_type=jnp.float32
    )
    key_new = rotary(key_raw, lengths).astype(jnp.bfloat16)
    mixed_latent = attend(
        query_latent,
        query_rope,
        latent_new,
        key_new,
        latent_cache,
        rope_cache,
        lengths,
        score_scale,
    )
    head_out = jnp.einsum(
        "rhl,hlv->rhv", mixed_latent, w_value_up, preferred_element_type=jnp.float32
    ).astype(jnp.bfloat16)
    heads_flat = head_out.reshape(row_count, -1)
    section_index = lax.axis_index("section")
    first_row = section_index * quarter
    own_hidden = lax.dynamic_slice_in_dim(hidden, first_row, quarter, 0)
    own_ids = lax.dynamic_slice_in_dim(expert_ids, first_row, quarter, 0)
    own_weights = lax.dynamic_slice_in_dim(route_weights, first_row, quarter, 0)
    block_index = lax.axis_index("dev") * sections + section_index
    table = route_table(own_ids, own_weights, w_gate_up.shape[0] * devices, block_index)
    part = jnp.dot(heads_flat, w_out, preferred_element_type=jnp.float32)
    return expert_layer(part, own_hidden, ffn_gain, table, w_gate_up, w_down)


def solution(mesh):
    in_specs = (
        P("dev", None),
        P("dev"),
        P(),
        P(None, "section"),
        P(),
        P(),
        P(),
        P("section", None, None),
        P("section", None, None),
        P("section", None),
        P("dev", None, None),
        P("dev", None, None),
        P(),
        P("dev", None),
        P("dev", None),
        P("dev", None, "section", None),
        P("dev", "section", None),
    )
    out_specs = P("dev", None)
    return jax.shard_map(
        per_device, mesh=mesh, in_specs=in_specs, out_specs=out_specs, check_vma=False
    )
```

```python
import functools

import jax
import jax.numpy as jnp
from jax import lax
from jax.experimental import pallas as pl
from jax.experimental.pallas import tpu as pltpu
from jax.sharding import PartitionSpec as P

MOST = 2
MESH = pl.DeviceIdType.MESH


epsilon = 1e-06
far_below = -1e30


def rms_norm(values, norm_gain):
    mean_square = jnp.mean(values * values, axis=-1, keepdims=True)
    return values * lax.rsqrt(mean_square + epsilon) * norm_gain


def rotary(values, positions):
    half_width = values.shape[-1] // 2
    step_index = jnp.arange(half_width, dtype=jnp.float32)
    frequency = jnp.exp(-jnp.log(10000.0) * step_index / half_width)
    angles = positions.astype(jnp.float32)[:, None] * frequency[None, :]
    if values.ndim == 3:
        angles = angles[:, None, :]
    cosine = jnp.cos(angles)
    sine_part = jnp.sin(angles)
    first_half = values[..., :half_width]
    second = values[..., half_width:]
    return jnp.concatenate(
        [first_half * cosine - second * sine_part, second * cosine + first_half * sine_part],
        axis=-1,
    )


def route_table(own_ids, own_weights, experts, block_index):
    hit = own_ids[:, :, None] == jnp.arange(experts, dtype=jnp.int32)[None, None, :]
    dense = jnp.sum(jnp.where(hit, own_weights[:, :, None], 0.0), axis=1)
    routed = jnp.any(hit, axis=1).astype(jnp.int32)
    rank = jnp.cumsum(routed, axis=0) - routed
    slot = jnp.where(routed > 0, block_index * MOST + rank, -1)
    return jnp.concatenate([dense, slot.astype(jnp.float32)], axis=1)


def expert_kernel(
    sections,
    devices,
    part_ref,
    hidden_ref,
    gain_ref,
    table_ref,
    w_up_ref,
    w_down_ref,
    out_ref,
    w_up,
    w_down,
    part_in,
    middle,
    row_out,
    rows_all,
    tables,
    pick,
    mix,
    packed,
    expert_out,
    sum_out,
    sum_in,
    pair_in,
    pair_sum,
    own_out,
    finished,
    up_sem,
    down_sem,
    part_send,
    part_recv,
    table_send,
    table_recv,
    row_send,
    row_recv,
    sum_send,
    sum_recv,
    pair_send,
    pair_recv,
    done_send,
    done_recv,
):
    section = lax.axis_index("section")
    dev = lax.axis_index("dev")
    total = sections * devices
    me = dev * sections + section
    local = w_up.shape[0]
    rows = total * row_out.shape[0]
    width = row_out.shape[1]
    experts = tables.shape[2] // 2
    slots = packed.shape[0] // local
    f32 = jnp.float32

    def up_copy(e):
        return pltpu.make_async_copy(w_up_ref.at[e], w_up.at[e], up_sem.at[e])

    def down_copy(e):
        return pltpu.make_async_copy(w_down_ref.at[e], w_down.at[e], down_sem.at[e])

    def place(t):
        return (lax.rem(t, sections), t // sections)

    def to_all(source, landing, send_sem, recv_sem):
        def copy(i, here):
            t = lax.rem(me + i, total)
            return pltpu.make_async_remote_copy(
                src_ref=source(t),
                dst_ref=landing.at[here],
                send_sem=send_sem.at[i],
                recv_sem=recv_sem.at[here],
                device_id=place(t),
                device_id_type=MESH,
            )

        @pl.loop(1, total)
        def _(i):
            copy(i, me).start()

        def wait_recv():
            @pl.loop(1, total)
            def _(i):
                copy(i, lax.rem(me + i, total)).wait_recv()

        def wait_send():
            @pl.loop(1, total)
            def _(i):
                copy(i, me).wait_send()

        return wait_recv, wait_send

    def to_sections(source, landing, send_sem, recv_sem):
        def copy(i, here):
            t = lax.rem(section + i, sections)
            return pltpu.make_async_remote_copy(
                src_ref=source(t),
                dst_ref=landing.at[here],
                send_sem=send_sem.at[i],
                recv_sem=recv_sem.at[here],
                device_id=(t, dev),
                device_id_type=MESH,
            )

        for i in range(1, sections):
            copy(i, section).start()

        def wait_recv():
            for i in range(1, sections):
                copy(i, lax.rem(section + i, sections)).wait_recv()

        def wait_send():
            for i in range(1, sections):
                copy(i, section).wait_send()

        return wait_recv, wait_send

    @pl.loop(0, local)
    def _(e):
        up_copy(e).start()
        down_copy(e).start()

    barrier = pltpu.get_barrier_semaphore()

    @pl.loop(1, total)
    def _(i):
        pl.semaphore_signal(
            barrier, inc=1, device_id=place(lax.rem(me + i, total)), device_id_type=MESH
        )

    pl.semaphore_wait(barrier, total - 1)

    part_recv_all, part_send_all = to_sections(
        lambda t: part_ref.at[t], part_in, part_send, part_recv
    )
    table_recv_all, table_send_all = to_all(lambda t: table_ref, tables, table_send, table_recv)
    part_in[section] = part_ref[section]
    tables[me] = table_ref[...]
    part_recv_all()
    summed = part_in[0]
    for j in range(1, sections):
        summed = summed + part_in[j]
    middle_rows = (hidden_ref[...].astype(f32) + summed).astype(jnp.bfloat16).astype(f32)
    middle[...] = middle_rows
    normed_rows = rms_norm(middle_rows, gain_ref[...]).astype(jnp.bfloat16)
    row_out[...] = normed_rows
    rows_all[me] = normed_rows
    row_recv_all, row_send_all = to_all(lambda t: row_out, rows_all, row_send, row_recv)

    table_recv_all()
    table = tables[...].reshape(rows, 2 * experts)
    lane = lax.broadcasted_iota(jnp.int32, (rows, 2 * experts), 1)
    column = lax.broadcasted_iota(jnp.int32, (rows, local * slots), 1)
    slot_at = jnp.full((rows, local * slots), -1.0, f32)
    weight_at = jnp.zeros((rows, local * slots), f32)
    for e in range(local):
        expert = dev * local + e
        weight_col = jnp.sum(jnp.where(lane == expert, table, 0.0), axis=1, keepdims=True)
        slot_col = jnp.sum(jnp.where(lane == experts + expert, table, 0.0), axis=1, keepdims=True)
        slot_col = jnp.where(slot_col < 0.0, -1.0, slot_col + float(e * slots))
        inside = (column >= e * slots) & (column < (e + 1) * slots)
        slot_at = jnp.where(inside, slot_col, slot_at)
        weight_at = jnp.where(inside, weight_col, weight_at)
    chosen = column.astype(f32) == slot_at
    pick[...] = jnp.where(chosen, 1.0, 0.0).astype(jnp.bfloat16)
    mix[...] = jnp.where(chosen, weight_at, 0.0).astype(jnp.bfloat16)

    row_recv_all()
    tile = 512

    @pl.loop(0, width // tile)
    def _(c):
        span = pl.ds(pl.multiple_of(c * tile, tile), tile)
        block = rows_all[:, :, span].astype(f32).reshape(rows, tile).astype(jnp.bfloat16)
        packed[:, span] = lax.dot_general(
            pick[...], block, (((0,), (0,)), ((), ())), preferred_element_type=f32
        ).astype(jnp.bfloat16)

    @pl.loop(0, local)
    def _(e):
        span = pl.ds(pl.multiple_of(e * slots, slots), slots)
        up_copy(e).wait()
        slot_rows = packed[span, :]
        flat = (((1,), (1,)), ((), ()))
        gate = lax.dot_general(slot_rows, w_up[e, 0], flat, preferred_element_type=f32)
        lift = lax.dot_general(slot_rows, w_up[e, 1], flat, preferred_element_type=f32)
        activated = (gate / (1.0 + jnp.exp(-gate)) * lift).astype(jnp.bfloat16)
        down_copy(e).wait()
        expert_out[span, :] = jnp.dot(
            activated, w_down[e], preferred_element_type=f32
        ).astype(jnp.bfloat16)

    @pl.loop(0, width // tile)
    def _(c):
        span = pl.ds(pl.multiple_of(c * tile, tile), tile)
        mixed = jnp.dot(mix[...], expert_out[:, span], preferred_element_type=f32)
        sum_out[:, :, span] = mixed.reshape(total, rows // total, tile).astype(jnp.bfloat16)

    core = lax.rem(dev, 2)
    pairs = devices // 2
    own_pair = dev // 2
    partner = (section, dev + 1 - 2 * core)

    def pair_copy(k):
        z = lax.rem(own_pair + 1 + k, pairs)
        source = (2 * z + 1 - core) * sections
        return pltpu.make_async_remote_copy(
            src_ref=sum_out.at[pl.ds(source, sections)],
            dst_ref=pair_in.at[z],
            send_sem=pair_send.at[k],
            recv_sem=pair_recv.at[k],
            device_id=partner,
            device_id_type=MESH,
        )

    def block_copy(z, t, here, slot):
        return pltpu.make_async_remote_copy(
            src_ref=pair_sum.at[z, t],
            dst_ref=sum_in.at[here],
            send_sem=sum_send.at[slot],
            recv_sem=sum_recv.at[here],
            device_id=(t, 2 * z + core),
            device_id_type=MESH,
        )

    here = own_pair * sections + section

    @pl.loop(0, pairs)
    def _(k):
        pair_copy(k).start()

    def add_pair(k):
        z = lax.rem(own_pair + 1 + k, pairs)
        pair_copy(k).wait_recv()
        mine = sum_out[pl.ds((2 * z + core) * sections, sections)].astype(f32)
        pair_sum[z] = (mine + pair_in[z].astype(f32)).astype(jnp.bfloat16)
        return z

    @pl.loop(0, pairs - 1)
    def _(k):
        z = add_pair(k)

        @pl.loop(0, sections)
        def _(j):
            t = lax.rem(section + j, sections)
            block_copy(z, t, here, z * sections + t).start()

    add_pair(pairs - 1)

    @pl.loop(1, sections)
    def _(j):
        t = lax.rem(section + j, sections)
        block_copy(own_pair, t, here, own_pair * sections + t).start()

    sum_in[here] = pair_sum[own_pair, section]
    part_send_all()
    table_send_all()
    row_send_all()
    half = pairs * sections

    @pl.loop(1, half)
    def _(i):
        t = lax.rem(here + i, half)
        block_copy(t // sections, lax.rem(t, sections), t, t).wait_recv()

    result = (middle[...] + jnp.sum(sum_in[...].astype(f32), axis=0)).astype(jnp.bfloat16)
    own_out[...] = result
    finished[section] = result
    done_recv_all, done_send_all = to_sections(
        lambda t: own_out, finished, done_send, done_recv
    )

    @pl.loop(1, half)
    def _(i):
        t = lax.rem(here + i, half)
        block_copy(t // sections, lax.rem(t, sections), here, t).wait_send()

    @pl.loop(0, pairs)
    def _(k):
        pair_copy(k).wait_send()

    done_recv_all()
    out_ref[...] = finished[...]
    done_send_all()


def expert_layer(part, own_hidden, ffn_gain, table, w_gate_up, w_down):
    sections = lax.axis_size("section")
    devices = lax.axis_size("dev")
    total = sections * devices
    quarter, width = own_hidden.shape
    local, _, units, _ = w_gate_up.shape
    slots = total * MOST
    rows = total * quarter
    bf16, f32 = jnp.bfloat16, jnp.float32
    vmem = pl.BlockSpec(memory_space=pltpu.VMEM)
    anywhere = pl.BlockSpec(memory_space=pl.ANY)
    sems = lambda count: pltpu.SemaphoreType.DMA((count,))
    out = pl.pallas_call(
        functools.partial(expert_kernel, sections, devices),
        out_shape=jax.ShapeDtypeStruct((sections, quarter, width), bf16),
        in_specs=[vmem] * 4 + [anywhere] * 2,
        out_specs=vmem,
        scratch_shapes=[
            pltpu.VMEM(w_gate_up.shape, bf16),
            pltpu.VMEM(w_down.shape, bf16),
            pltpu.VMEM((sections, quarter, width), f32),
            pltpu.VMEM((quarter, width), f32),
            pltpu.VMEM((quarter, width), bf16),
            pltpu.VMEM((total, quarter, width), bf16),
            pltpu.VMEM((total,) + table.shape, f32),
            pltpu.VMEM((rows, local * slots), bf16),
            pltpu.VMEM((rows, local * slots), bf16),
            pltpu.VMEM((local * slots, width), bf16),
            pltpu.VMEM((local * slots, width), bf16),
            pltpu.VMEM((total, quarter, width), bf16),
            pltpu.VMEM((total // 2, quarter, width), bf16),
            pltpu.VMEM((devices // 2, sections, quarter, width), bf16),
            pltpu.VMEM((devices // 2, sections, quarter, width), bf16),
            pltpu.VMEM((quarter, width), bf16),
            pltpu.VMEM((sections, quarter, width), bf16),
            sems(local),
            sems(local),
            sems(sections),
            sems(sections),
            sems(total),
            sems(total),
            sems(total),
            sems(total),
            sems(total // 2),
            sems(total // 2),
            sems(devices // 2),
            sems(devices // 2),
            sems(sections),
            sems(sections),
        ],
        compiler_params=pltpu.CompilerParams(
            collective_id=0, has_side_effects=True, vmem_limit_bytes=58 * 1024 * 1024
        ),
    )(
        part.reshape(sections, quarter, width),
        own_hidden,
        ffn_gain.reshape(1, width),
        table,
        w_gate_up,
        w_down,
    )
    return out.reshape(sections * quarter, width)


def attend(
    query_latent, query_rope, latent_new, key_new, latent_cache, rope_cache, lengths, score_scale
):
    scores = jnp.einsum(
        "rhl,rtl->rht", query_latent, latent_cache, preferred_element_type=jnp.float32
    )
    scores = scores + jnp.einsum(
        "rhp,rpt->rht", query_rope, rope_cache, preferred_element_type=jnp.float32
    )
    scores = scores * score_scale
    self_score = jnp.einsum(
        "rhl,rl->rh", query_latent, latent_new, preferred_element_type=jnp.float32
    )
    self_score = (
        self_score
        + jnp.einsum("rhp,rp->rh", query_rope, key_new, preferred_element_type=jnp.float32)
    ) * score_scale
    places = jnp.arange(latent_cache.shape[1], dtype=jnp.int32)
    valid_mask = places[None, None, :] < lengths[:, None, None]
    masked = jnp.where(valid_mask, scores, far_below)
    peak_score = jnp.maximum(jnp.max(masked, axis=2), self_score)
    weights = jnp.where(valid_mask, jnp.exp(masked - peak_score[:, :, None]), 0.0)
    self_weight = jnp.exp(self_score - peak_score)
    totals = jnp.sum(weights, axis=2) + self_weight
    prob_cache = (weights / totals[:, :, None]).astype(jnp.bfloat16)
    prob_self = (self_weight / totals).astype(jnp.bfloat16)
    mixed = jnp.einsum("rht,rtl->rhl", prob_cache, latent_cache, preferred_element_type=jnp.float32)
    mixed = (
        mixed
        + prob_self.astype(jnp.float32)[:, :, None] * latent_new.astype(jnp.float32)[:, None, :]
    )
    return mixed.astype(jnp.bfloat16)


def per_device(
    hidden,
    lengths,
    attn_gain,
    w_query,
    w_latent,
    latent_gain,
    w_rope_key,
    w_key_up,
    w_value_up,
    w_out,
    latent_cache,
    rope_cache,
    ffn_gain,
    expert_ids,
    route_weights,
    w_gate_up,
    w_down,
):
    sections = lax.axis_size("section")
    devices = lax.axis_size("dev")
    row_count = hidden.shape[0]
    quarter = row_count // sections
    head_local = w_key_up.shape[0]
    nope_width = w_key_up.shape[2]
    rope_width = w_rope_key.shape[0]
    score_scale = (nope_width + rope_width) ** (-0.5)
    normed = rms_norm(hidden.astype(jnp.float32), attn_gain).astype(jnp.bfloat16)
    queries = jnp.dot(normed, w_query, preferred_element_type=jnp.float32).astype(jnp.bfloat16)
    queries = queries.reshape(row_count, head_local, nope_width + rope_width)
    query_rope = rotary(queries[:, :, nope_width:].astype(jnp.float32), lengths).astype(
        jnp.bfloat16
    )
    query_latent = jnp.einsum(
        "rhn,hln->rhl", queries[:, :, :nope_width], w_key_up, preferred_element_type=jnp.float32
    ).astype(jnp.bfloat16)
    latent_new = rms_norm(
        jnp.dot(normed, w_latent, preferred_element_type=jnp.float32), latent_gain
    ).astype(jnp.bfloat16)
    key_raw = lax.dot_general(
        normed, w_rope_key, (((1,), (1,)), ((), ())), preferred_element_type=jnp.float32
    )
    key_new = rotary(key_raw, lengths).astype(jnp.bfloat16)
    mixed_latent = attend(
        query_latent,
        query_rope,
        latent_new,
        key_new,
        latent_cache,
        rope_cache,
        lengths,
        score_scale,
    )
    head_out = jnp.einsum(
        "rhl,hlv->rhv", mixed_latent, w_value_up, preferred_element_type=jnp.float32
    ).astype(jnp.bfloat16)
    heads_flat = head_out.reshape(row_count, -1)
    section_index = lax.axis_index("section")
    first_row = section_index * quarter
    own_hidden = lax.dynamic_slice_in_dim(hidden, first_row, quarter, 0)
    own_ids = lax.dynamic_slice_in_dim(expert_ids, first_row, quarter, 0)
    own_weights = lax.dynamic_slice_in_dim(route_weights, first_row, quarter, 0)
    block_index = lax.axis_index("dev") * sections + section_index
    table = route_table(own_ids, own_weights, w_gate_up.shape[0] * devices, block_index)
    part = jnp.dot(heads_flat, w_out, preferred_element_type=jnp.float32)
    return expert_layer(part, own_hidden, ffn_gain, table, w_gate_up, w_down)


def solution(mesh):
    in_specs = (
        P("dev", None),
        P("dev"),
        P(),
        P(None, "section"),
        P(),
        P(),
        P(),
        P("section", None, None),
        P("section", None, None),
        P("section", None),
        P("dev", None, None),
        P("dev", None, None),
        P(),
        P("dev", None),
        P("dev", None),
        P("dev", None, "section", None),
        P("dev", "section", None),
    )
    out_specs = P("dev", None)
    return jax.shard_map(
        per_device, mesh=mesh, in_specs=in_specs, out_specs=out_specs, check_vma=False
    )
```
